32 devices in a mesh: ctx: 8 (over z, y), tp: 4 (over x, core).
Axes of the slice: x: 2, y: 2, z: 4, core: 2. Of those that a mesh axis runs over, the one named last changes fastest.
Arguments:
- queries: bfloat16 [1024, 4096], P('ctx', 'tp'), may hold values from -64 to 64
- encoded_key_rows: bfloat16 [1024, 2048], P('ctx', 'tp'), may hold values from -6 to 6
- value_matrix_rows: bfloat16 [1024, 2048], P('ctx', 'tp'), may hold values from -6 to 6
- out_weight: bfloat16 [4096, 5376], P('tp'), may hold values from -0.5 to 0.5
- cotangent: bfloat16 [1024, 5376], P(('ctx', 'tp')), may hold values from -1.5 to 1.5
- doc_lengths: int32 [16], replicated, may hold values from 1 to 256, 1024 in all
Outputs:
- layer_out: bfloat16 [1024, 5376], P(('ctx', 'tp'))
- query_grad: bfloat16 [1024, 4096], P('ctx', 'tp')
- key_grad: bfloat16 [1024, 2048], P('ctx', 'tp')
- value_grad: bfloat16 [1024, 2048], P('ctx', 'tp')
The draws below stay inside these ranges and needn't reach their ends.
Inputs may be any that keep to these rules, and one draw needn't show every extreme that they name: `doc_lengths`: they sum to 1024, and the longest document has exactly 256 tokens.
All inputs are finite; a program needn't handle non-finite values.
Results may differ from the reference program's by a relative error of at most 0.017.
Values may be sent and summed in bfloat16 or wider, within the bound.
No kernel may reach another device: no remote copies, remote signals or barrier semaphores. Data moves between devices by JAX's collectives and lax.ppermute only.
A program may use at most 64 MiB of HBM per device.

```python
import math
import jax
import jax.numpy as jnp
import numpy as np
from jax import lax

D = 5376
QUERY_HEADS = 32
KEY_VALUE_HEADS = 16
HEAD_SIZE = 128
WINDOW_SPAN = 1024
NDOC = 16
TOKENS_PER_SHARD = 128
PACKED_TOKENS = 1024
DOC_MOST = 256
N_TP = 4


def joint_draw(key):
    starting_key = jax.random.fold_in(key, 7101)
    query_key = jax.random.fold_in(key, 7102)
    key_offset = jnp.clip(jax.random.normal(starting_key, (PACKED_TOKENS, KEY_VALUE_HEADS, HEAD_SIZE), jnp.float32), -6.0, 6.0)
    query_offset = jnp.clip(2.0 * jax.random.normal(query_key, (PACKED_TOKENS, QUERY_HEADS, HEAD_SIZE), jnp.float32), -12.0, 12.0)
    return (query_offset.reshape(PACKED_TOKENS, QUERY_HEADS * HEAD_SIZE), key_offset.reshape(PACKED_TOKENS, KEY_VALUE_HEADS * HEAD_SIZE))


def draw_queries(key, part):
    return joint_draw(key)[0].astype(jnp.bfloat16)


def draw_encoded_key_rows(key, part):
    return joint_draw(key)[1].astype(jnp.bfloat16)


def block_scale(own_key, dims, cuts, smallest, top_value):
    gain, own = 1.0, jax.random.fold_in(own_key, 6)
    for axis_at, parts in cuts:
        draws = jnp.exp(jax.random.uniform(jax.random.fold_in(own, axis_at), (parts,), jnp.float32, smallest / len(cuts), top_value / len(cuts)))
        gain = gain * jnp.repeat(draws, dims[axis_at] // parts).reshape([-1 if axis == axis_at else 1 for axis in range(len(dims))])
    return gain


def profile(count, total, most, slope):
    weights = [(1 << 20) // math.isqrt(grade ** slope) + 1 for grade in range(2, count + 1)]
    rest, given = total - most - (count - 1), [1] * (count - 1)
    while rest > 0:
        free = [i for i in range(count - 1) if given[i] < most]
        whole, remaining = sum([weights[i] for i in free]), rest
        for i in free:
            addition = min(most - given[i], max(1, remaining * weights[i] // whole), rest)
            given[i] = given[i] + addition
            rest = rest - addition
    return np.array([most] + given)


def uneven(stream_key, number_of, total, reach, skew):
    if number_of == 2:
        one = jax.random.randint(stream_key, (), max(1, total - reach), min(reach, total - 1) + 1)
        return jnp.stack([one, total - one])
    tallies = jnp.asarray(profile(number_of, total, reach, skew), jnp.int32)
    pairs = (number_of - 1) // 2
    giver, taker = tallies[1:1 + 2 * pairs:2], tallies[2:2 + 2 * pairs:2]
    margin = jnp.minimum(giver - 1, reach - taker)
    shifted = jax.random.randint(jax.random.fold_in(stream_key, 1), (pairs,), 0, 1 << 20) % (margin + 1)
    tallies = tallies.at[1:1 + 2 * pairs:2].set(giver - shifted).at[2:2 + 2 * pairs:2].set(taker + shifted)
    return tallies[jax.random.permutation(jax.random.fold_in(stream_key, 2), number_of)]


def centred(rng, shape, deviation, limit, pieces=(), kind=jnp.bfloat16):
    gain = block_scale(rng, shape, pieces, -0.22, 0.18) if pieces else 1.0
    result = jax.random.normal(rng, shape, jnp.float32) * deviation * gain
    return jnp.minimum(jnp.maximum(result, -limit), limit).astype(kind)


def setup_inputs(seed: int = 0) -> dict:
    streams_of = jax.random.split(jax.random.key(seed), 7)
    queries = draw_queries(jax.random.fold_in(streams_of[6], 71), 0)
    encoded_key_rows = draw_encoded_key_rows(jax.random.fold_in(streams_of[6], 71), 0)
    value_matrix_rows = centred(streams_of[2], (PACKED_TOKENS, KEY_VALUE_HEADS * HEAD_SIZE), 1.0, 6.0, ((0, 8), (1, 4)))
    out_weight = centred(streams_of[3], (QUERY_HEADS * HEAD_SIZE, D), (QUERY_HEADS * HEAD_SIZE // 32) ** -0.5, 0.5, ((0, 4),))
    cotangent = centred(streams_of[4], (PACKED_TOKENS, D), 0.25, 1.5, ((0, 32),))
    doc_lengths = uneven(streams_of[5], NDOC, PACKED_TOKENS, DOC_MOST, 2).astype(jnp.int32)
    return dict(queries=queries, encoded_key_rows=encoded_key_rows, value_matrix_rows=value_matrix_rows, out_weight=out_weight, cotangent=cotangent, doc_lengths=doc_lengths)


def doc_index(positions, doc_ends):
    return jnp.sum((positions[:, None] >= doc_ends[None, :]).astype(jnp.int32), axis=1)


def allowed_pairs(query_pos, key_pos, doc_lengths):
    doc_ends = jnp.cumsum(doc_lengths).astype(jnp.int32)
    same_doc = doc_index(query_pos, doc_ends)[:, None] == doc_index(key_pos, doc_ends)[None, :]
    distance = query_pos[:, None] - key_pos[None, :]
    return same_doc & (distance >= 0) & (distance < WINDOW_SPAN) & (key_pos[None, :] >= 0)


def softmax_rows(scores, allowed):
    masked = jnp.where(allowed[None, None], scores, -jnp.inf)
    peak = jnp.max(masked, axis=-1, keepdims=True)
    unnorm = jnp.exp(masked - peak)
    return unnorm / jnp.sum(unnorm, axis=-1, keepdims=True)


def reference(queries, encoded_key_rows, value_matrix_rows, out_weight, cotangent, doc_lengths):
    query_group_size = QUERY_HEADS // KEY_VALUE_HEADS
    score_scale = (D / QUERY_HEADS) ** -0.5
    pad_amount = jnp.zeros((WINDOW_SPAN, KEY_VALUE_HEADS * HEAD_SIZE), encoded_key_rows.dtype)
    padded_key_rows = jnp.concatenate([pad_amount, encoded_key_rows], axis=0)
    padded_value_rows = jnp.concatenate([pad_amount, value_matrix_rows], axis=0)
    block_ids = jnp.arange(PACKED_TOKENS // TOKENS_PER_SHARD, dtype=jnp.int32)

    def block_probs(block):
        leading_row = block * TOKENS_PER_SHARD
        query_block = lax.dynamic_slice_in_dim(queries, leading_row, TOKENS_PER_SHARD, 0).reshape(TOKENS_PER_SHARD, KEY_VALUE_HEADS, query_group_size, HEAD_SIZE).astype(jnp.float32)
        key_block = lax.dynamic_slice_in_dim(padded_key_rows, leading_row, WINDOW_SPAN + TOKENS_PER_SHARD, 0).reshape(WINDOW_SPAN + TOKENS_PER_SHARD, KEY_VALUE_HEADS, HEAD_SIZE).astype(jnp.float32)
        value_block = lax.dynamic_slice_in_dim(padded_value_rows, leading_row, WINDOW_SPAN + TOKENS_PER_SHARD, 0).reshape(WINDOW_SPAN + TOKENS_PER_SHARD, KEY_VALUE_HEADS, HEAD_SIZE).astype(jnp.float32)
        query_pos = leading_row + jnp.arange(TOKENS_PER_SHARD, dtype=jnp.int32)
        key_pos = leading_row - WINDOW_SPAN + jnp.arange(WINDOW_SPAN + TOKENS_PER_SHARD, dtype=jnp.int32)
        scores = jnp.einsum('pkgd,nkd->kgpn', query_block, key_block) * score_scale
        probs = softmax_rows(scores, allowed_pairs(query_pos, key_pos, doc_lengths))
        return query_block, key_block, value_block, probs

    def forward_block(block):
        query_block, key_block, value_block, probs = block_probs(block)
        probabilities_narrow = probs.astype(jnp.bfloat16).astype(jnp.float32)
        attended = jnp.einsum('kgpn,nkd->pkgd', probabilities_narrow, value_block)
        return attended.astype(jnp.bfloat16).reshape(TOKENS_PER_SHARD, QUERY_HEADS * HEAD_SIZE)

    attended = lax.map(forward_block, block_ids).reshape(PACKED_TOKENS, QUERY_HEADS * HEAD_SIZE)
    col_width = QUERY_HEADS * HEAD_SIZE // N_TP
    summed = jnp.zeros((PACKED_TOKENS, D), jnp.float32)
    for group in range(N_TP):
        partial_value = jnp.dot(attended[:, group * col_width:(group + 1) * col_width],
                          out_weight[group * col_width:(group + 1) * col_width],
                          preferred_element_type=jnp.float32).astype(jnp.bfloat16)
        partial_value = lax.optimization_barrier(partial_value)
        summed = summed + partial_value.astype(jnp.float32)
    layer_out = summed.astype(jnp.bfloat16)

    attended_output_grad = lax.dot_general(cotangent, out_weight, (((1,), (1,)), ((), ())),
                                    preferred_element_type=jnp.float32).astype(jnp.bfloat16)

    def backward_block(carry, block):
        key_acc, value_acc = carry
        query_block, key_block, value_block, probs = block_probs(block)
        leading_row = block * TOKENS_PER_SHARD
        probabilities_narrow = probs.astype(jnp.bfloat16)
        gradient_block = lax.dynamic_slice_in_dim(attended_output_grad, leading_row, TOKENS_PER_SHARD, 0).reshape(TOKENS_PER_SHARD, KEY_VALUE_HEADS, query_group_size, HEAD_SIZE).astype(jnp.float32)
        prob_grad = jnp.einsum('pkgd,nkd->kgpn', gradient_block, value_block)
        row_delta = jnp.sum(probs * prob_grad, axis=-1, keepdims=True)
        score_gradient = (probs * (prob_grad - row_delta) * score_scale).astype(jnp.bfloat16).astype(jnp.float32)
        query_grad = jnp.einsum('kgpn,nkd->pkgd', score_gradient, key_block).astype(jnp.bfloat16).reshape(TOKENS_PER_SHARD, QUERY_HEADS * HEAD_SIZE)
        key_gradient_term = jnp.einsum('hofw,fhot->wht', score_gradient, query_block).reshape(WINDOW_SPAN + TOKENS_PER_SHARD, KEY_VALUE_HEADS * HEAD_SIZE)
        value_gradient_term = jnp.einsum('hofw,fhot->wht', probabilities_narrow.astype(jnp.float32), gradient_block).reshape(WINDOW_SPAN + TOKENS_PER_SHARD, KEY_VALUE_HEADS * HEAD_SIZE)
        key_acc = lax.dynamic_update_slice_in_dim(
            key_acc, lax.dynamic_slice_in_dim(key_acc, leading_row, WINDOW_SPAN + TOKENS_PER_SHARD, 0) + key_gradient_term, leading_row, 0)
        value_acc = lax.dynamic_update_slice_in_dim(
            value_acc, lax.dynamic_slice_in_dim(value_acc, leading_row, WINDOW_SPAN + TOKENS_PER_SHARD, 0) + value_gradient_term, leading_row, 0)
        return (key_acc, value_acc), query_grad

    zeroed_accumulator = jnp.zeros((WINDOW_SPAN + PACKED_TOKENS, KEY_VALUE_HEADS * HEAD_SIZE), jnp.float32)
    (key_acc, value_acc), query_grad = lax.scan(backward_block, (zeroed_accumulator, zeroed_accumulator), block_ids)
    query_grad = query_grad.reshape(PACKED_TOKENS, QUERY_HEADS * HEAD_SIZE)
    key_grad = key_acc[WINDOW_SPAN:].astype(jnp.bfloat16)
    value_grad = value_acc[WINDOW_SPAN:].astype(jnp.bfloat16)
    return (layer_out, query_grad, key_grad, value_grad)
```

```python
import jax
import jax.numpy as jnp
from jax import lax
from jax.sharding import PartitionSpec as P

D = 5376
QUERY_HEADS = 32
KEY_VALUE_HEADS = 16
HEAD_SIZE = 128
WINDOW_SPAN = 1024
LONGEST_SHARE = 4


def passed_along(value, axis, steps):
    count = lax.axis_size(axis)
    leading, last = (max(0, -steps), min(count, count - steps))
    return lax.ppermute(value, axis, [(source, source + steps) for source in range(leading, last)])


def doc_index(positions, doc_ends):
    return jnp.sum((positions[:, None] >= doc_ends[None, :]).astype(jnp.int32), axis=1)


def allowed_pairs(query_pos, key_pos, doc_lengths):
    doc_ends = jnp.cumsum(doc_lengths)
    same_doc = doc_index(query_pos, doc_ends)[:, None] == doc_index(key_pos, doc_ends)[None, :]
    distance = query_pos[:, None] - key_pos[None, :]
    return same_doc & (distance >= 0) & (distance < WINDOW_SPAN) & (key_pos[None, :] >= 0)


def softmax_rows(scores, allowed):
    masked = jnp.where(allowed[None, None], scores, -jnp.inf)
    peak = jnp.max(masked, axis=-1, keepdims=True)
    unnorm = jnp.exp(masked - peak)
    return unnorm / jnp.sum(unnorm, axis=-1, keepdims=True)


def all_gather_tp(value, axis):
    count = lax.axis_size(axis)
    me = lax.axis_index(axis)
    block = value[None]
    step = count // 2
    held = [value]
    offsets = [0]
    while step >= 1:
        got = lax.ppermute(jnp.stack(held), axis, [(d, d ^ step) for d in range(count)])
        held = held + [got[j] for j in range(len(held))]
        offsets = offsets + [o ^ step for o in offsets]
        step //= 2
    stacked = jnp.stack(held)
    inverse = [offsets.index(o) for o in range(count)]
    by_offset = stacked[jnp.array(inverse)]
    order = jnp.bitwise_xor(jnp.arange(count, dtype=jnp.int32), me)
    ordered = by_offset[order]
    return ordered.reshape((count * value.shape[0],) + value.shape[1:])


def reduce_scatter_tp(value, axis):
    count = lax.axis_size(axis)
    me = lax.axis_index(axis)
    rows = value.shape[0] // count
    blocks = value.reshape((count, rows) + value.shape[1:])
    order = jnp.bitwise_xor(jnp.arange(count, dtype=jnp.int32), me)
    blocks = blocks[order]
    step = 1
    while step < count:
        pairs = blocks.reshape((-1, 2) + blocks.shape[1:])
        got = lax.ppermute(pairs[:, 1].astype(jnp.bfloat16), axis, [(d, d ^ step) for d in range(count)])
        blocks = pairs[:, 0].astype(jnp.float32) + got.astype(jnp.float32)
        step *= 2
    return blocks[0].astype(jnp.bfloat16)


def local(queries, encoded_key_rows, value_matrix_rows, out_weight, cotangent, doc_lengths):
    tok_rows = queries.shape[0]
    kv_cols = encoded_key_rows.shape[1]
    heads_kv = kv_cols // HEAD_SIZE
    query_group_size = QUERY_HEADS // KEY_VALUE_HEADS
    tokens = tok_rows * lax.axis_size("ctx")
    longest = tokens // LONGEST_SHARE
    reach_count = -(-(min(WINDOW_SPAN, longest) - 1) // tok_rows)
    score_scale = (D / QUERY_HEADS) ** (-0.5)
    device = lax.axis_index("ctx")
    key_value = jnp.concatenate([encoded_key_rows, value_matrix_rows], axis=1)
    behind = [passed_along(key_value, "ctx", distance) for distance in range(reach_count, 0, -1)]
    gathered = jnp.concatenate(behind + [key_value], axis=0)
    key_count = gathered.shape[0]
    keys_all = gathered[:, :kv_cols].reshape(key_count, heads_kv, HEAD_SIZE)
    values_all = gathered[:, kv_cols:].reshape(key_count, heads_kv, HEAD_SIZE)
    query_pos = device * tok_rows + jnp.arange(tok_rows, dtype=jnp.int32)
    key_pos = (device - reach_count) * tok_rows + jnp.arange(key_count, dtype=jnp.int32)
    allowed = allowed_pairs(query_pos, key_pos, doc_lengths)
    query_four = queries.reshape(tok_rows, heads_kv, query_group_size, HEAD_SIZE)
    scores = (
        jnp.einsum("pkgd,nkd->kgpn", query_four, keys_all, preferred_element_type=jnp.float32)
        * score_scale
    )
    probs = softmax_rows(scores, allowed)
    probabilities_narrow = probs.astype(jnp.bfloat16)
    attended = (
        jnp.einsum(
            "kgpn,nkd->pkgd", probabilities_narrow, values_all, preferred_element_type=jnp.float32
        )
        .astype(jnp.bfloat16)
        .reshape(tok_rows, heads_kv * query_group_size * HEAD_SIZE)
    )
    layer_out = reduce_scatter_tp(
        jnp.dot(attended, out_weight, preferred_element_type=jnp.float32).astype(jnp.bfloat16),
        "tp",
    )
    attended_output_grad = lax.dot_general(
        all_gather_tp(cotangent, "tp"),
        out_weight,
        (((1,), (1,)), ((), ())),
        preferred_element_type=jnp.float32,
    ).astype(jnp.bfloat16)
    grad_four = attended_output_grad.reshape(tok_rows, heads_kv, query_group_size, HEAD_SIZE)
    prob_grad = jnp.einsum(
        "pkgd,nkd->kgpn", grad_four, values_all, preferred_element_type=jnp.float32
    )
    row_delta = jnp.sum(probs * prob_grad, axis=-1, keepdims=True)
    score_gradient = (probs * (prob_grad - row_delta) * score_scale).astype(jnp.bfloat16)
    query_grad = (
        jnp.einsum("kgpn,nkd->pkgd", score_gradient, keys_all, preferred_element_type=jnp.float32)
        .astype(jnp.bfloat16)
        .reshape(tok_rows, queries.shape[1])
    )
    key_terms = jnp.einsum(
        "hofw,fhot->wht", score_gradient, query_four, preferred_element_type=jnp.float32
    ).reshape(key_count, kv_cols)
    value_terms = jnp.einsum(
        "hofw,fhot->wht", probabilities_narrow, grad_four, preferred_element_type=jnp.float32
    ).reshape(key_count, kv_cols)
    grads = jnp.concatenate([key_terms, value_terms], axis=1)
    own_grad = grads[reach_count * tok_rows :]
    for distance in range(1, reach_count + 1):
        gradient_block = grads[
            (reach_count - distance) * tok_rows : (reach_count - distance + 1) * tok_rows
        ]
        own_grad = own_grad + passed_along(
            gradient_block.astype(jnp.bfloat16), "ctx", -distance
        ).astype(gradient_block.dtype)
    key_grad = own_grad[:, :kv_cols].astype(jnp.bfloat16)
    value_grad = own_grad[:, kv_cols:].astype(jnp.bfloat16)
    return (layer_out, query_grad, key_grad, value_grad)


def solution(mesh):
    in_specs = (
        P("ctx", "tp"),
        P("ctx", "tp"),
        P("ctx", "tp"),
        P("tp", None),
        P(("ctx", "tp"), None),
        P(),
    )
    out_specs = (P(("ctx", "tp"), None), P("ctx", "tp"), P("ctx", "tp"), P("ctx", "tp"))
    return jax.shard_map(local, mesh=mesh, in_specs=in_specs, out_specs=out_specs, check_vma=False)
```

```python
import functools

import jax
import jax.numpy as jnp
from jax import lax
from jax.experimental import pallas as pl
from jax.experimental.pallas import tpu as pltpu
from jax.sharding import PartitionSpec as P

D = 5376
QUERY_HEADS = 32
KEY_VALUE_HEADS = 16
HEAD_SIZE = 128
WINDOW_SPAN = 1024
LONGEST_SHARE = 4

BF16 = jnp.bfloat16
F32 = jnp.float32
VMEM_LIMIT = 40 * 1024 * 1024


def passed_along(value, axis, steps):
    count = lax.axis_size(axis)
    leading, last = (max(0, -steps), min(count, count - steps))
    return lax.ppermute(value, axis, [(source, source + steps) for source in range(leading, last)])


def swapped(value, axis, step):
    return lax.ppermute(value, axis, [(d, d ^ step) for d in range(lax.axis_size(axis))])


def column_tile(width, most):
    return max(t for t in range(128, most + 1, 128) if width % t == 0)


def dot_nt(a, b):
    return lax.dot_general(a, b, (((1,), (1,)), ((), ())), preferred_element_type=F32)


def dot_nn(a, b):
    return lax.dot_general(a, b, (((1,), (0,)), ((), ())), preferred_element_type=F32)


def dot_tn(a, b):
    return lax.dot_general(a, b, (((0,), (0,)), ((), ())), preferred_element_type=F32)


def attended_grad_kernel(offsets, rows, me_ref, *refs):
    blocks, w_ref, out_ref, lhs_ref = refs[:-3], refs[-3], refs[-2], refs[-1]

    @pl.when(pl.program_id(0) == 0)
    def _():
        for slot, block in enumerate(blocks):
            lhs_ref[slot * rows : (slot + 1) * rows, :] = block[...]

    product = dot_nt(lhs_ref[...], w_ref[...]).astype(BF16)
    for slot, offset in enumerate(offsets):
        start = pl.multiple_of((me_ref[0] ^ offset) * rows, rows)
        out_ref[pl.ds(start, rows), :] = product[slot * rows : (slot + 1) * rows]


def attended_grad_of(blocks, offsets, out_weight, me):
    rows, width = blocks[0].shape
    heads_width = out_weight.shape[0]
    tokens = rows * len(blocks)
    tile = min(heads_width, 128)
    whole = pl.BlockSpec((rows, width), lambda i, *_: (0, 0))
    return pl.pallas_call(
        functools.partial(attended_grad_kernel, offsets, rows),
        out_shape=jax.ShapeDtypeStruct((tokens, heads_width), BF16),
        grid_spec=pltpu.PrefetchScalarGridSpec(
            num_scalar_prefetch=1,
            grid=(heads_width // tile,),
            in_specs=[whole] * len(blocks) + [pl.BlockSpec((tile, width), lambda i, *_: (i, 0))],
            out_specs=pl.BlockSpec((tokens, tile), lambda i, *_: (0, i)),
            scratch_shapes=[pltpu.VMEM((tokens, width), BF16)],
        ),
        compiler_params=pltpu.CompilerParams(vmem_limit_bytes=VMEM_LIMIT),
        cost_estimate=pl.CostEstimate(
            flops=2 * tokens * heads_width * width,
            bytes_accessed=2 * (heads_width * width + tokens * width + tokens * heads_width),
            transcendentals=0,
        ),
        name="attended_grad",
    )(me, *blocks, out_weight)


def attention_kernel(reach, kv_heads, group, scale, span, ctx_ref, lengths_ref, q_ref, g_ref, *refs):
    kv_refs = refs[: reach + 1]
    att_ref, dq_ref, own_ref = refs[reach + 1 : reach + 4]
    far_refs = refs[reach + 4 :]
    rows = q_ref.shape[0]
    width = kv_heads * HEAD_SIZE
    keys = (reach + 1) * rows
    first_query = ctx_ref[0] * rows
    query_pos = first_query + lax.broadcasted_iota(jnp.int32, (8, rows), 1)
    low = jnp.maximum(query_pos - (span - 1), 0)
    end = jnp.int32(0)
    for d in range(lengths_ref.shape[0]):
        end = end + lengths_ref[d]
        low = jnp.maximum(low, jnp.where(query_pos >= end, end, 0))
    low = low[:1]
    query_pos = query_pos[:1]
    key_pos = first_query - reach * rows + lax.broadcasted_iota(jnp.int32, (keys, rows), 0)
    allowed = (key_pos >= low) & (key_pos <= query_pos)
    bias = jnp.where(allowed, 0.0, -jnp.inf).astype(F32)
    bias = jnp.concatenate([bias] * group, axis=1)

    for head in range(kv_heads):
        columns = slice(head * HEAD_SIZE, (head + 1) * HEAD_SIZE)
        value_columns = slice(width + head * HEAD_SIZE, width + (head + 1) * HEAD_SIZE)
        k = jnp.concatenate([r[:, columns] for r in kv_refs], axis=0)
        v = jnp.concatenate([r[:, value_columns] for r in kv_refs], axis=0)
        group_columns = [
            slice((head * group + g) * HEAD_SIZE, (head * group + g + 1) * HEAD_SIZE) for g in range(group)
        ]
        q = jnp.concatenate([q_ref[:, c] for c in group_columns], axis=0)
        grad = jnp.concatenate([g_ref[:, c] for c in group_columns], axis=0)
        scores = dot_nt(k, q) * scale + bias
        unnorm = jnp.exp(scores - jnp.max(scores, axis=0, keepdims=True))
        probs = unnorm * (1.0 / jnp.sum(unnorm, axis=0, keepdims=True))
        probs_low = probs.astype(BF16)
        prob_grad = dot_nt(v, grad)
        delta = jnp.sum(probs * prob_grad, axis=0, keepdims=True)
        score_grad = (probs * (prob_grad - delta) * scale).astype(BF16)
        attended = dot_tn(probs_low, v).astype(BF16)
        query_grad = dot_tn(score_grad, k).astype(BF16)
        for g, c in enumerate(group_columns):
            att_ref[:, c] = attended[g * rows : (g + 1) * rows]
            dq_ref[:, c] = query_grad[g * rows : (g + 1) * rows]
        dk = dot_nn(score_grad, q)
        dv = dot_nn(probs_low, grad)
        for j, ref in enumerate(far_refs):
            ref[:, columns] = dk[j * rows : (j + 1) * rows].astype(ref.dtype)
            ref[:, value_columns] = dv[j * rows : (j + 1) * rows].astype(ref.dtype)
        own_ref[:, columns] = dk[reach * rows :]
        own_ref[:, value_columns] = dv[reach * rows :]


def attention_of(queries, grad, key_value_blocks, ctx, doc_lengths, scale, span):
    rows, q_width = queries.shape
    kv_width = key_value_blocks[0].shape[1]
    reach = len(key_value_blocks) - 1
    kv_heads = kv_width // (2 * HEAD_SIZE)
    group = q_width // (kv_heads * HEAD_SIZE)
    vmem = pl.BlockSpec(memory_space=pltpu.VMEM)
    smem = pl.BlockSpec(memory_space=pltpu.SMEM)
    keys = (reach + 1) * rows
    return pl.pallas_call(
        functools.partial(attention_kernel, reach, kv_heads, group, scale, span),
        out_shape=[
            jax.ShapeDtypeStruct((rows, q_width), BF16),
            jax.ShapeDtypeStruct((rows, q_width), BF16),
            jax.ShapeDtypeStruct((rows, kv_width), F32),
        ]
        + [jax.ShapeDtypeStruct((rows, kv_width), BF16)] * reach,
        in_specs=[smem, smem] + [vmem] * (reach + 3),
        out_specs=[vmem] * (reach + 3),
        compiler_params=pltpu.CompilerParams(vmem_limit_bytes=VMEM_LIMIT),
        cost_estimate=pl.CostEstimate(
            flops=12 * keys * rows * q_width,
            bytes_accessed=2 * (4 * rows * q_width + 2 * keys * kv_width),
            transcendentals=keys * rows * q_width // HEAD_SIZE,
        ),
        name="attention",
    )(ctx, doc_lengths, queries, grad, *key_value_blocks)


def projection_kernel(offsets, rows, me_ref, att_ref, w_ref, keep_ref, send_ref, lhs_ref):
    @pl.when(pl.program_id(0) == 0)
    def _():
        for slot, offset in enumerate(offsets):
            start = pl.multiple_of((me_ref[0] ^ offset) * rows, rows)
            lhs_ref[slot * rows : (slot + 1) * rows, :] = att_ref[pl.ds(start, rows), :]

    product = dot_nn(lhs_ref[...], w_ref[...])
    half = keep_ref.shape[0]
    keep_ref[...] = product[:half]
    send_ref[...] = product[half:].astype(send_ref.dtype)


def projection_of(attended, out_weight, me, offsets):
    tokens, heads_width = attended.shape
    width = out_weight.shape[1]
    rows = tokens // len(offsets)
    half = tokens // 2
    tile = column_tile(width, 1024)
    return pl.pallas_call(
        functools.partial(projection_kernel, offsets, rows),
        out_shape=[
            jax.ShapeDtypeStruct((half, width), F32),
            jax.ShapeDtypeStruct((half, width), BF16),
        ],
        grid_spec=pltpu.PrefetchScalarGridSpec(
            num_scalar_prefetch=1,
            grid=(width // tile,),
            in_specs=[
                pl.BlockSpec((tokens, heads_width), lambda i, *_: (0, 0)),
                pl.BlockSpec((heads_width, tile), lambda i, *_: (0, i)),
            ],
            out_specs=[
                pl.BlockSpec((half, tile), lambda i, *_: (0, i)),
                pl.BlockSpec((half, tile), lambda i, *_: (0, i)),
            ],
            scratch_shapes=[pltpu.VMEM((tokens, heads_width), BF16)],
        ),
        compiler_params=pltpu.CompilerParams(vmem_limit_bytes=VMEM_LIMIT),
        cost_estimate=pl.CostEstimate(
            flops=2 * tokens * heads_width * width,
            bytes_accessed=2 * (heads_width * width + 2 * tokens * width),
            transcendentals=0,
        ),
        name="projection",
    )(me, attended, out_weight)


def local(queries, encoded_key_rows, value_matrix_rows, out_weight, cotangent, doc_lengths):
    tok_rows = queries.shape[0]
    kv_cols = encoded_key_rows.shape[1]
    tokens = tok_rows * lax.axis_size("ctx")
    reach = -(-(min(WINDOW_SPAN, tokens // LONGEST_SHARE) - 1) // tok_rows)
    score_scale = (D / QUERY_HEADS) ** (-0.5)
    members = lax.axis_size("tp")
    rows = tok_rows // members
    me = lax.axis_index("tp").astype(jnp.int32).reshape(1)
    ctx = lax.axis_index("ctx").astype(jnp.int32).reshape(1)

    key_value = jnp.concatenate([encoded_key_rows, value_matrix_rows], axis=1)
    behind = [passed_along(key_value, "ctx", distance) for distance in range(reach, 0, -1)]

    blocks, offsets, step = [cotangent], [0], members // 2
    while step:
        blocks = blocks + [swapped(b, "tp", step) for b in blocks]
        offsets = offsets + [o ^ step for o in offsets]
        step //= 2
    grad = attended_grad_of(blocks, offsets, out_weight, me)

    attended, query_grad, own, *far = attention_of(
        queries, grad, behind + [key_value], ctx, doc_lengths, score_scale, WINDOW_SPAN
    )

    order = [j for j in range(members) if j % 2 == 0] + [j for j in range(members) if j % 2 == 1]
    keep, send = projection_of(attended, out_weight, me, order)
    held = [j for j in order if j % 2 == 0]
    step = 1
    while True:
        total = keep + swapped(send, "tp", step).astype(F32)
        step *= 2
        if step == members:
            break
        kept = [i for i, j in enumerate(held) if not j & step]
        sent = [i for i, j in enumerate(held) if j & step]
        keep = jnp.concatenate([total[i * rows : (i + 1) * rows] for i in kept], axis=0)
        send = jnp.concatenate([total[i * rows : (i + 1) * rows] for i in sent], axis=0).astype(BF16)
        held = [held[i] for i in kept]
    layer_out = total.astype(BF16)

    for distance, block in zip(range(reach, 0, -1), far):
        own = own + passed_along(block, "ctx", -distance).astype(F32)
    return (layer_out, query_grad, own[:, :kv_cols].astype(BF16), own[:, kv_cols:].astype(BF16))


def solution(mesh):
    in_specs = (
        P("ctx", "tp"),
        P("ctx", "tp"),
        P("ctx", "tp"),
        P("tp", None),
        P(("ctx", "tp"), None),
        P(),
    )
    out_specs = (P(("ctx", "tp"), None), P("ctx", "tp"), P("ctx", "tp"), P("ctx", "tp"))
    return jax.shard_map(local, mesh=mesh, in_specs=in_specs, out_specs=out_specs, check_vma=False)
```
